32 devices in a mesh: gx: 4 (over z), gy: 2 (over x), gz: 4 (over y, core).
Axes of the slice: x: 2, y: 2, z: 4, core: 2. Of those that a mesh axis runs over, the one named last changes fastest.
Arguments:
- weights: bfloat16 [32, 32, 32, 2, 8, 512], P('gx', 'gy', 'gz'), may hold values from -6 to 6
- angles: float32 [3, 32, 32, 32, 512], P(None, 'gx', 'gy', 'gz'), may hold values from -3.140625 to 3.140625
- translation: bfloat16 [8, 512, 512], replicated, may hold values from -0.09375 to 0.09375
Outputs:
- transformed: bfloat16 [32, 32, 32, 2, 8, 512], P('gx', 'gy', 'gz')
The draws below stay inside these ranges and needn't reach their ends.
All inputs are finite; a program needn't handle non-finite values.
Results may differ from the reference program's by a relative error of at most 0.025.
Values may be sent and summed in bfloat16 or wider, within the bound.
A program may use at most 128 MiB of HBM per device.

```python
import jax
import jax.numpy as jnp
from jax import lax

PX = 32
PY = 32
PZ = 32
CHEB = 512
RHS = 8
LEVELS = 3


def block_scale(key, extent, cuts, smallest, top_value):
    def one(dim, blocks):
        heights = jax.random.uniform(jax.random.fold_in(jax.random.fold_in(key, 6), dim), (blocks,), jnp.float32, smallest / len(cuts), top_value / len(cuts))
        return jnp.repeat(jnp.exp(heights), extent[dim] // blocks).reshape((-1,) + (1,) * (len(extent) - dim - 1))

    level = one(*cuts[0])
    for cut in cuts[1:]:
        level = level * one(*cut)
    return level


def scatter_about(own_key, dims, scale, most, pieces=(), dtype=jnp.bfloat16):
    loudness = block_scale(own_key, dims, pieces, -0.22, 0.18) if pieces else 1.0
    array = jax.random.normal(own_key, dims, jnp.float32) * scale * loudness
    return jnp.minimum(jnp.maximum(array, -most), most).astype(dtype)


def setup_inputs(seed: int = 0) -> dict:
    streams_of = jax.random.split(jax.random.key(seed), 4)
    weights = scatter_about(streams_of[0], (PX, PY, PZ, 2, RHS, CHEB), 1.0, 6.0, ((0, 4), (1, 2), (2, 4)))
    angles = jnp.clip(jax.random.uniform(streams_of[1], (LEVELS, PX, PY, PZ, CHEB), jnp.float32, -3.140625, 3.140625), -3.140625, 3.140625)
    translation = scatter_about(streams_of[2], (8, CHEB, CHEB), (8 * CHEB) ** -0.5, 0.09375)
    return {"weights": weights, "angles": angles, "translation": translation}


def rotate_phase(current, angle):
    real_part = current[:, :, :, 0].astype(jnp.float32)
    imag_part = current[:, :, :, 1].astype(jnp.float32)
    cosine = jnp.cos(angle)[:, :, :, None, :]
    sine = jnp.sin(angle)[:, :, :, None, :]
    rotated_re = real_part * cosine - imag_part * sine
    rotated_im = real_part * sine + imag_part * cosine
    return jnp.stack([rotated_re, rotated_im], axis=3).astype(jnp.bfloat16)


def fold_local(child_terms, dim_pos, low_span):
    dims_shape = child_terms.shape
    count = dims_shape[dim_pos]
    split = child_terms.reshape(dims_shape[:dim_pos] + (count // (2 * low_span), 2, low_span) + dims_shape[dim_pos + 1:])
    first = jnp.take(split, 0, axis=dim_pos + 1).astype(jnp.float32)
    second = jnp.take(split, 1, axis=dim_pos + 1).astype(jnp.float32)
    added = (first + second).astype(jnp.bfloat16)
    return added.reshape(dims_shape[:dim_pos] + (count // 2,) + dims_shape[dim_pos + 1:])


def insert_bit(lower, upper, dim_pos, low_span):
    dims_shape = lower.shape
    count = dims_shape[dim_pos]
    inner_shape = dims_shape[:dim_pos] + (count // low_span, low_span) + dims_shape[dim_pos + 1:]
    stacked = jnp.stack([lower.reshape(inner_shape), upper.reshape(inner_shape)], axis=dim_pos + 1)
    return stacked.reshape(dims_shape[:dim_pos] + (2 * count,) + dims_shape[dim_pos + 1:])


def translate_all(summed, translation, local_dims, chosen_bits):
    if not local_dims:
        orient = 4 * chosen_bits[0] + 2 * chosen_bits[1] + chosen_bits[2]
        matrix = lax.dynamic_index_in_dim(translation, orient, 0, keepdims=False)
        rows = summed.reshape(-1, summed.shape[-1])
        result = jnp.dot(rows, matrix, preferred_element_type=jnp.float32)
        return result.astype(jnp.bfloat16).reshape(summed.shape)
    dim_pos, low_span = local_dims[0]
    halves = []
    for t in (0, 1):
        picked = dict(chosen_bits)
        picked[dim_pos] = t
        halves.append(translate_all(summed, translation, local_dims[1:], picked))
    return insert_bit(halves[0], halves[1], dim_pos, low_span)


def reference(weights, angles, translation):
    current = weights
    size_list = (PX, PY, PZ)
    for level_idx in range(LEVELS):
        child_terms = rotate_phase(current, angles[level_idx])
        local_dims = []
        for d in range(3):
            low_span = 2 ** (size_list[d].bit_length() - 2 - level_idx)
            child_terms = fold_local(child_terms, d, low_span)
            local_dims.append((d, low_span))
        current = translate_all(child_terms, translation, local_dims, dict())
    return current
```

```python
import jax
import jax.numpy as jnp
from jax import lax
from jax.experimental import pallas as pl
from jax.experimental.pallas import tpu as pltpu
from jax.sharding import PartitionSpec as P

LEVELS = 3
AXES = ("gx", "gy", "gz")


def sincos(angle):
    half = angle * 0.5
    sq = half * half
    sin_half = -1.0 / 39916800.0
    for c in (1.0 / 362880.0, -1.0 / 5040.0, 1.0 / 120.0, -1.0 / 6.0, 1.0):
        sin_half = sin_half * sq + c
    sin_half = sin_half * half
    cos_half = 1.0 / 479001600.0
    for c in (-1.0 / 3628800.0, 1.0 / 40320.0, -1.0 / 720.0, 1.0 / 24.0, -0.5, 1.0):
        cos_half = cos_half * sq + c
    return 1.0 - 2.0 * sin_half * sin_half, 2.0 * sin_half * cos_half


def halve_sum(terms, axis_name, dim):
    count = lax.axis_size(axis_name)
    bit = lax.axis_index(axis_name) // (count // 2)
    mine = lax.dynamic_index_in_dim(terms, bit, dim, keepdims=True)
    theirs = lax.dynamic_index_in_dim(terms, 1 - bit, dim, keepdims=True)
    pairs = [(i, (i + count // 2) % count) for i in range(count)]
    got = lax.ppermute(theirs, axis_name, pairs)
    return (mine.astype(jnp.float32) + got.astype(jnp.float32)).astype(jnp.bfloat16)


def exchange_low(terms, axis_name, dim):
    count = lax.axis_size(axis_name)
    low = count // 2
    if low == 1:
        return terms
    groups = [[h * low + i for i in range(low)] for h in range(2)]
    return lax.all_to_all(
        terms, axis_name, split_axis=dim, concat_axis=dim, axis_index_groups=groups, tiled=True
    )


def rotate_sum(current, angle):
    cosine, sine = sincos(angle.astype(jnp.float32))
    cosine = cosine[..., None, :]
    sine = sine[..., None, :]
    re = current[0].astype(jnp.float32)
    im = current[1].astype(jnp.float32)
    return re * cosine - im * sine, re * sine + im * cosine


def shards(weights, angles, translation):
    counts = [lax.axis_size(a) for a in AXES]
    count_x, count_y, count_z = counts
    devices = count_x * count_y * count_z
    count_yz = count_y * count_z
    top = 2**LEVELS
    hx, hy, hz = (top // c for c in counts)
    lx, ly, lz = (weights.shape[0] // hx, weights.shape[1] // hy, weights.shape[2] // hz)
    rhs, cheb = weights.shape[4], weights.shape[5]
    blocks = lx * ly * lz
    share = blocks * rhs // devices
    block_share = max(1, blocks // devices)
    rhs_share = share // block_share
    repeat = max(1, devices // blocks)
    C = hx * hy * hz

    ph = angles[1:].astype(jnp.bfloat16)
    ph = ph.reshape(LEVELS - 1, hx, lx, hy, ly, hz, lz, cheb).transpose(1, 3, 5, 0, 2, 4, 6, 7)
    ph = ph.reshape(1, 1, hx, hy, hz, LEVELS - 1, blocks, 1, cheb)
    ph = jnp.broadcast_to(ph, ph.shape[:7] + (repeat, cheb))
    ph = ph.reshape(
        1, 1, hx, hy, hz, LEVELS - 1, count_x, blocks * repeat // count_x, cheb
    )
    ph = lax.all_to_all(ph, "gx", split_axis=6, concat_axis=0, tiled=True)
    ph = lax.all_to_all(ph, ("gy", "gz"), split_axis=7, concat_axis=1, tiled=True)
    ph = ph.reshape(count_x, count_y, count_z, hx, hy, hz, LEVELS - 1, block_share, cheb)
    ph = ph.transpose(6, 0, 3, 1, 4, 2, 5, 7, 8)
    ph = ph.reshape(LEVELS - 1, top, top, top, block_share, cheb)

    parts = [
        v.reshape(C, 2, count_x // 2, 2, count_y // 2, 2, count_z // 2, share, cheb)
        for v in first_rotate(weights, angles[0], (lx, ly, lz))
    ]
    where = {"gx": 1, "gy": 3, "gz": 5}
    orders = [("gx", "gy", "gz"), ("gy", "gz", "gx"), ("gz", "gx", "gy")]
    cuts = [C * i // 3 for i in range(4)]
    streams = {}
    for p in range(2):
        for k in range(3):
            if cuts[k + 1] > cuts[k]:
                streams[p, k] = parts[p][cuts[k] : cuts[k + 1]]
    for step in range(3):
        for p, k in list(streams):
            name = orders[k][step]
            streams[p, k] = halve_sum(streams[p, k], name, where[name])
    both = jnp.stack(
        [jnp.concatenate([streams[p, k] for k in range(3) if (p, k) in streams]) for p in range(2)]
    )
    both = both.reshape(2, C, count_x // 2, count_y // 2, count_z // 2, share, cheb)
    for dim, name in ((2, "gx"), (3, "gy"), (4, "gz")):
        both = exchange_low(both, name, dim)
    both = both.reshape(
        2, hx, hy, hz, count_x // 2, count_y // 2, count_z // 2, block_share, rhs_share, cheb
    )
    summed = both.transpose(0, 4, 1, 5, 2, 6, 3, 7, 8, 9)
    q = top // 2
    summed = summed.reshape(2, q * q * q * share, cheb)

    def translate(s):
        return jnp.einsum(
            "crk,tkn->ctrn", s, translation, preferred_element_type=jnp.float32
        ).astype(jnp.bfloat16)

    tail = (block_share, rhs_share, cheb)
    w = translate(summed)
    w = w.reshape((2, 2, 2, 2, 2, 2, 2, 2, 2, 2) + tail)
    ang = ph[0].reshape((2,) * 9 + (block_share, cheb))
    ang = ang.transpose(0, 3, 6, 1, 2, 4, 5, 7, 8, 9, 10)
    r, i = rotate_sum(w, ang)
    summed = jnp.stack([r.sum((3, 5, 7)), i.sum((3, 5, 7))]).astype(jnp.bfloat16)
    w = translate(summed.reshape(2, q * q * q * share, cheb))
    w = w.reshape((2,) + (2,) * 9 + tail)
    ang = ph[1].reshape((2,) * 9 + (block_share, cheb))
    ang = ang.transpose(1, 4, 7, 0, 3, 6, 2, 5, 8, 9, 10)
    r, i = rotate_sum(w, ang)
    summed = jnp.stack([r.sum((6, 7, 8)), i.sum((6, 7, 8))]).astype(jnp.bfloat16)
    summed = summed.transpose(4, 1, 5, 2, 6, 3, 0, 7, 8, 9)
    summed = summed.reshape(q, q, q, 2, share, cheb)
    keep = []
    for d, c in enumerate(counts):
        if c > q:
            summed = jnp.repeat(summed, c // q, axis=d)
        keep.append(max(1, q // c))
    kx, ky, kz = keep
    leaving = summed.reshape(count_x, kx, count_y, ky, count_z, kz, 2, share, cheb)
    leaving = leaving.transpose(0, 2, 4, 1, 3, 5, 6, 7, 8)
    leaving = leaving.reshape(count_x, count_yz, kx, ky, kz, 2, 1, share, cheb)
    back = lax.all_to_all(leaving, "gx", split_axis=0, concat_axis=6, tiled=True)
    back = lax.all_to_all(back, ("gy", "gz"), split_axis=1, concat_axis=7, tiled=True)
    back = back.reshape(kx, ky, kz, 2, lx, ly, lz, rhs, cheb)

    mats = translation.reshape(2, 2, 2, cheb, cheb)
    for d, (c, name) in enumerate(zip(counts, AXES)):
        if c > q:
            mats = lax.dynamic_index_in_dim(mats, lax.axis_index(name) % 2, d, keepdims=True)
    return last_translate(back, mats, weights.shape)


def last_kernel(e_ref, t_ref, o_ref):
    rows = e_ref[0, 0]
    lx, ly, kz, nz, m, cheb = (o_ref.shape[1],) + tuple(o_ref.shape[3:])
    for z in range(nz):
        r = jnp.dot(rows, t_ref[0, 0, z], preferred_element_type=jnp.float32)
        o_ref[0, :, 0, :, :, z] = r.astype(jnp.bfloat16).reshape(lx, ly, kz, m, cheb)


def last_translate(back, mats, out_shape):
    kx, ky, kz, _, lx, ly, lz, rhs, cheb = back.shape
    nx, ny, nz = mats.shape[:3]
    m = lz * 2 * rhs
    rows = back.transpose(0, 1, 4, 5, 2, 6, 3, 7, 8).reshape(kx, ky, lx * ly * kz * m, cheb)
    out = pl.pallas_call(
        last_kernel,
        grid=(nx, ny, kx, ky),
        in_specs=[
            pl.BlockSpec((1, 1, lx * ly * kz * m, cheb), lambda x, y, a, b: (a, b, 0, 0)),
            pl.BlockSpec((1, 1, nz, cheb, cheb), lambda x, y, a, b: (x, y, 0, 0, 0)),
        ],
        out_specs=pl.BlockSpec(
            (1, lx, 1, ly, kz, nz, m, cheb),
            lambda x, y, a, b: (a * nx + x, 0, b * ny + y, 0, 0, 0, 0, 0),
        ),
        out_shape=jax.ShapeDtypeStruct(
            (kx * nx, lx, ky * ny, ly, kz, nz, m, cheb), jnp.bfloat16
        ),
        compiler_params=pltpu.CompilerParams(vmem_limit_bytes=40 * 2**20),
        name="last_translate",
    )(rows, mats)
    return out.reshape(out_shape)


def first_kernel(w_ref, a_ref, re_ref, im_ref, cos_ref, sin_ref):
    ly, count_z = a_ref.shape[3], a_ref.shape[4]
    lz = re_ref.shape[5]
    cosine, sine = sincos(a_ref[0, 0, 0])
    cos_ref[...] = cosine
    sin_ref[...] = sine

    @pl.loop(0, ly)
    def _(l):
        for z in range(count_z):
            c = cos_ref[l, z : z + 1, :]
            s = sin_ref[l, z : z + 1, :]
            re = w_ref[0, 0, 0, l, z, 0].astype(jnp.float32)
            im = w_ref[0, 0, 0, l, z, 1].astype(jnp.float32)
            re_ref[0, 0, z // lz, 0, l, z % lz] = (re * c - im * s).astype(jnp.bfloat16)
            im_ref[0, 0, z // lz, 0, l, z % lz] = (re * s + im * c).astype(jnp.bfloat16)


def first_rotate(weights, angle, low):
    lx, ly, lz = low
    sx, sy, sz, _, rhs, cheb = weights.shape
    hx, hy, hz = sx // lx, sy // ly, sz // lz
    shape = (hx, hy, hz, lx, ly, lz, rhs, cheb)
    out = jax.ShapeDtypeStruct(shape, jnp.bfloat16)
    spec = pl.BlockSpec(
        (1, 1, hz, 1, ly, lz, rhs, cheb), lambda a, x, b: (a, b, 0, x, 0, 0, 0, 0)
    )
    return pl.pallas_call(
        first_kernel,
        grid=(hx, lx, hy),
        in_specs=[
            pl.BlockSpec(
                (1, 1, 1, ly, sz, 2, rhs, cheb), lambda a, x, b: (a, x, b, 0, 0, 0, 0, 0)
            ),
            pl.BlockSpec((1, 1, 1, ly, sz, cheb), lambda a, x, b: (a, x, b, 0, 0, 0)),
        ],
        out_specs=[spec, spec],
        out_shape=[out, out],
        scratch_shapes=[pltpu.VMEM((ly, sz, cheb), jnp.float32)] * 2,
        compiler_params=pltpu.CompilerParams(vmem_limit_bytes=40 * 2**20),
        name="first_rotate",
    )(
        weights.reshape(hx, lx, hy, ly, sz, 2, rhs, cheb),
        angle.reshape(hx, lx, hy, ly, sz, cheb),
    )


def solution(mesh):
    in_specs = (P("gx", "gy", "gz", None, None, None), P(None, "gx", "gy", "gz", None), P())
    out_specs = P("gx", "gy", "gz", None, None, None)
    return jax.shard_map(shards, mesh=mesh, in_specs=in_specs, out_specs=out_specs, check_vma=False)
```
